128 devices in a mesh: dp: 8 (over z, y_lo), pocket: 16 (over x, y_hi, core).
Axes of the slice: x: 4, y: 4 (y_hi: 2, y_lo: 2; y = y_hi * 2 + y_lo), z: 4, core: 2. Of those that a mesh axis runs over, the one named last changes fastest.
Arguments:
- atoms: bfloat16 [1024, 128, 768], P(('dp', 'pocket')), may hold values from -6 to 6
- distance_bins: int32 [1024, 128, 128], P(('dp', 'pocket')), may hold values from 0 to 31
- bonds: int32 [1024, 128, 128], P(('dp', 'pocket')), may hold values 0 or 1
- molecule: int32 [1024, 128], P(('dp', 'pocket')), may hold values from 0 to 3, never falling along the last dimension, each value on 1 to 64 neighbouring positions
- block_counts: int32 [8, 16], P('dp', 'pocket'), may hold values from 1 to 8, as said below
- block_scaffold: int32 [1024], replicated, may hold values from 0 to 8191
- pocket_ids: int32 [8192, 4], replicated, may hold values from 0 to 15, as said below
- pocket_keys: bfloat16 [2048, 768], P('pocket'), may hold values from -6 to 6
- pocket_values: bfloat16 [2048, 768], P('pocket'), may hold values from -6 to 6
- pocket_bias: bfloat16 [12, 2048], P(None, 'pocket'), may hold values from -4 to 320
- bin_table: float32 [12, 32], replicated, may hold values from -4 to 320
- bond_weight: float32 [12], replicated, may hold values from 0.5 to 2.5
- w_query: bfloat16 [768, 768], replicated, may hold values from -0.21875 to 0.21875
- w_key: bfloat16 [768, 768], replicated, may hold values from -0.21875 to 0.21875
- w_value: bfloat16 [768, 768], replicated, may hold values from -0.21875 to 0.21875
- w_out: bfloat16 [768, 768], replicated, may hold values from -0.21875 to 0.21875
- w_cross_query: bfloat16 [768, 768], replicated, may hold values from -0.21875 to 0.21875
- w_cross_out: bfloat16 [768, 768], replicated, may hold values from -0.21875 to 0.21875
- cotangent: bfloat16 [512, 128, 768], P(('dp', 'pocket')), may hold values from -6 to 6
Outputs:
- updated: bfloat16 [512, 128, 768], P(('dp', 'pocket'))
- weight_grads: bfloat16 [6, 768, 768], replicated
The draws below stay inside these ranges and needn't reach their ends.
Inputs may be any that keep to these rules, and one draw needn't show every extreme that they name: `block_counts`: every column sums to 32, and in every column one device has exactly 8 live blocks. `pocket_ids`: each row names 4 different pocket blocks.
All inputs are finite; a program needn't handle non-finite values. No bound on the sum of `bonds` on one device may be relied on, other than what follows from the above.
Results may differ from the reference program's by a relative error of at most 0.012.
The reference program's roundings to bfloat16 on the way count: a program that leaves them out, or rounds other values in their place, can miss the bound.
Values may be sent and summed in bfloat16 or wider, within the bound.
No kernel may reach another device: no remote copies, remote signals or barrier semaphores. Data moves between devices by JAX's collectives and lax.ppermute only.
A program may use at most 128 MiB of HBM per device.

```python
import math
import jax
import jax.numpy as jnp
import numpy as np
from jax import lax

D = 768
H = 12
A = 128
NBINS = 32
MOLS = 4
KP = 4
SCAFFOLDS = 8192
BAL = 4
CAP = 8
DP_DEVS = 8
POCKET_DEVS = 16
SLOTS = 1024
BLOCKS = 512
ROWS = 65536
PBLK = 16
PATOMS = 2048


def draw_block_counts(key, part):
    heavy_key = jax.random.fold_in(key, 11)
    fill_key = jax.random.fold_in(key, 12)
    device_rows = lax.broadcasted_iota(jnp.int32, (DP_DEVS, POCKET_DEVS), 0)
    heavy = jax.random.randint(heavy_key, (1, POCKET_DEVS), 0, DP_DEVS)
    start_counts = jnp.where(device_rows == heavy, CAP, 1).astype(jnp.int32)
    extra_units = DP_DEVS * BAL - CAP - (DP_DEVS - 1)

    def add_one(step_index, current):
        draws = jax.random.randint(jax.random.fold_in(fill_key, step_index), (DP_DEVS, POCKET_DEVS), 0, 1 << 20)
        ranked = draws * DP_DEVS + device_rows
        ranked = jnp.where(current < CAP, ranked, -1)
        best_score = jnp.max(ranked, axis=0, keepdims=True)
        return current + (ranked == best_score).astype(jnp.int32)
    return lax.fori_loop(0, extra_units, add_one, start_counts)


def draw_pocket_ids(key, part):
    draws = jax.random.randint(jax.random.fold_in(key, 21), (SCAFFOLDS, PBLK), 0, 1 << 16)
    ranked = draws * PBLK + lax.broadcasted_iota(jnp.int32, (SCAFFOLDS, PBLK), 1)
    ordering = jnp.argsort(ranked, axis=1, stable=True)
    return ordering[:, :KP].astype(jnp.int32)


def draw_bin_table(key, part):
    base_key = jax.random.fold_in(key, 31)
    values = jnp.clip(jax.random.normal(base_key, (H, NBINS), jnp.float32), -4.0, 4.0)
    return values


def draw_pocket_bias(key, part):
    base_key = jax.random.fold_in(key, 51)
    values = jnp.clip(jax.random.normal(base_key, (H, PATOMS), jnp.float32), -4.0, 4.0)
    return values.astype(jnp.bfloat16)


def set_ends(values, key, least, largest):
    longest = values.shape.index(max(values.shape))
    spots = []
    for shift in (0, 1):
        where = [jax.random.randint(jax.random.fold_in(key, axis), (), 0, length) for axis, length in enumerate(values.shape)]
        where[longest] = (where[longest] + shift) % values.shape[longest]
        spots.append(tuple(where))
    return values.at[spots[0]].set(least).at[spots[1]].set(largest)


def block_scale(stream_key, shape, split, low, high):
    factor_of, own = 1.0, jax.random.fold_in(stream_key, 6)
    for dim, shards_of in split:
        steps = jnp.exp(jax.random.uniform(jax.random.fold_in(own, dim), (shards_of,), jnp.float32, low / len(split), high / len(split)))
        factor_of = factor_of * jnp.repeat(steps, shape[dim] // shards_of).reshape([-1 if axis == dim else 1 for axis in range(len(shape))])
    return factor_of


def profile(amount, total, reach, skew):
    loads = [(1 << 20) // math.isqrt(grade ** skew) + 1 for grade in range(2, amount + 1)]
    surplus, given = total - reach - (amount - 1), [1] * (amount - 1)
    while surplus > 0:
        movable = [i for i in range(amount - 1) if given[i] < reach]
        mass, left = sum([loads[i] for i in movable]), surplus
        for i in movable:
            more = min(reach - given[i], max(1, left * loads[i] // mass), surplus)
            given[i] = given[i] + more
            surplus = surplus - more
    return np.array([reach] + given)


def ragged(own_key, count, total, most, slope):
    if count == 2:
        one = jax.random.randint(own_key, (), max(1, total - most), min(most, total - 1) + 1)
        return jnp.stack([one, total - one])
    lengths = jnp.asarray(profile(count, total, most, slope), jnp.int32)
    couples = (count - 1) // 2
    source_of, receiver = lengths[1:1 + 2 * couples:2], lengths[2:2 + 2 * couples:2]
    margin = jnp.minimum(source_of - 1, most - receiver)
    shifted = jax.random.randint(jax.random.fold_in(own_key, 1), (couples,), 0, 1 << 20) % (margin + 1)
    lengths = lengths.at[1:1 + 2 * couples:2].set(source_of - shifted).at[2:2 + 2 * couples:2].set(receiver + shifted)
    return lengths[jax.random.permutation(jax.random.fold_in(own_key, 2), count)]


def scatter_about(rng, shape, scale, limit, shards=(), kind=jnp.bfloat16):
    values = jax.random.normal(rng, shape, jnp.float32) * scale
    if len(shards) > 0:
        values = block_scale(rng, shape, shards, -0.22, 0.18) * values
    return jnp.clip(values, min=-limit, max=limit).astype(kind)


def setup_inputs(seed: int = 0) -> dict:
    seeds = jax.random.split(jax.random.key(seed), 20)
    atoms = scatter_about(seeds[0], (SLOTS, A, D), 1.0, 6.0, ((0, 128),))
    distance_bins = set_ends(jax.random.randint(seeds[1], (SLOTS, A, A), 0, NBINS), jax.random.fold_in(seeds[1], 1), 0, NBINS - 1).astype(jnp.int32)
    bonds = set_ends((jax.random.randint(seeds[2], (SLOTS, A, A), 0, 8) < 1).astype(jnp.int32), jax.random.fold_in(seeds[2], 1), 0, 1)
    molecule = jax.vmap(lambda own: jnp.searchsorted(jnp.cumsum(ragged(own, MOLS, A, A // 2, 2)), jnp.arange(A), side="right"))(jax.random.split(seeds[3], SLOTS)).reshape((SLOTS, A)).astype(jnp.int32)
    block_counts = draw_block_counts(jax.random.fold_in(seeds[19], 71), 0)
    block_scaffold = set_ends(jax.random.randint(seeds[5], (SLOTS,), 0, SCAFFOLDS), jax.random.fold_in(seeds[5], 1), 0, SCAFFOLDS - 1).astype(jnp.int32)
    pocket_ids = draw_pocket_ids(jax.random.fold_in(seeds[19], 71), 0)
    pocket_keys = scatter_about(seeds[7], (PATOMS, D), 1.0, 6.0, ((0, 16),))
    pocket_values = scatter_about(seeds[8], (PATOMS, D), 1.0, 6.0, ((0, 16),))
    pocket_bias = draw_pocket_bias(jax.random.fold_in(seeds[19], 71), 0)
    bin_table = draw_bin_table(jax.random.fold_in(seeds[19], 71), 0)
    bond_weight = jnp.clip(jax.random.uniform(seeds[11], (H,), jnp.float32, 0.5, 2.5), 0.5, 2.5)
    w_query = scatter_about(seeds[12], (D, D), D ** -0.5, 0.21875)
    w_key = scatter_about(seeds[13], (D, D), D ** -0.5, 0.21875)
    w_value = scatter_about(seeds[14], (D, D), D ** -0.5, 0.21875)
    w_out = scatter_about(seeds[15], (D, D), D ** -0.5, 0.21875)
    w_cross_query = scatter_about(seeds[16], (D, D), D ** -0.5, 0.21875)
    w_cross_out = scatter_about(seeds[17], (D, D), D ** -0.5, 0.21875)
    cotangent = scatter_about(seeds[18], (BLOCKS, A, D), 1.0, 6.0, ((0, 128),))
    return {"atoms": atoms, "distance_bins": distance_bins, "bonds": bonds, "molecule": molecule, "block_counts": block_counts, "block_scaffold": block_scaffold, "pocket_ids": pocket_ids, "pocket_keys": pocket_keys, "pocket_values": pocket_values, "pocket_bias": pocket_bias, "bin_table": bin_table, "bond_weight": bond_weight, "w_query": w_query, "w_key": w_key, "w_value": w_value, "w_out": w_out, "w_cross_query": w_cross_query, "w_cross_out": w_cross_out, "cotangent": cotangent}


masked_value = -30000.0

def pair_bias(bin_rows, bond_rows, molecule_rows, bin_table, bond_weight):
    bin_count = bin_table.shape[1]
    levels = lax.broadcasted_iota(jnp.int32, (1, 1, 1, bin_count), 3)
    one_hot = (bin_rows[..., None] == levels).astype(jnp.float32)
    looked_up = jnp.einsum('cijn,hn->chij', one_hot, bin_table.astype(jnp.float32), precision=lax.Precision.HIGHEST)
    bonded = looked_up + bond_weight.astype(jnp.float32)[None, :, None, None] * bond_rows[:, None, :, :].astype(jnp.float32)
    same_molecule = molecule_rows[:, None, :, None] == molecule_rows[:, None, None, :]
    return jnp.where(same_molecule, bonded, masked_value).astype(jnp.bfloat16)

def project_rows(left, weight):
    flat = left.reshape(-1, left.shape[-1])
    result = jnp.dot(flat, weight, preferred_element_type=jnp.float32)
    return result.reshape(left.shape[:-1] + (weight.shape[1],))

def project_back(left, weight):
    flat = left.reshape(-1, left.shape[-1])
    result = lax.dot_general(flat, weight, (((1,), (1,)), ((), ())), preferred_element_type=jnp.float32)
    return result.reshape(left.shape[:-1] + (weight.shape[0],))

def weight_product(left, right):
    return lax.dot_general(left.reshape(-1, left.shape[-1]), right.reshape(-1, right.shape[-1]), (((0,), (0,)), ((), ())), preferred_element_type=jnp.float32)

def softmax_rows(scores):
    highest = lax.optimization_barrier(jnp.max(scores, axis=-1, keepdims=True))
    expsum = jnp.exp(scores - highest)
    return expsum / lax.optimization_barrier(jnp.sum(expsum, axis=-1, keepdims=True))

def split_heads(matrix, heads):
    return matrix.reshape(matrix.shape[0], matrix.shape[1], heads, matrix.shape[2] // heads)

def einsum_wide(form, left, right):
    return jnp.einsum(form, left.astype(jnp.float32), right.astype(jnp.float32))

def layer_pass(block_atoms, block_bias, cross_keys, cross_values, cross_bias, cotangent_rows, weights, heads):
    w_query, w_key, w_value, w_out, w_cquery, w_cout = weights
    block_count, row_count, width = block_atoms.shape
    scale = 1.0 / math.sqrt(width // heads)
    query_rows = project_rows(block_atoms, w_query).astype(jnp.bfloat16)
    key_rows = project_rows(block_atoms, w_key).astype(jnp.bfloat16)
    value_rows = project_rows(block_atoms, w_value).astype(jnp.bfloat16)
    query_heads = split_heads(query_rows, heads)
    key_heads = split_heads(key_rows, heads)
    value_heads = split_heads(value_rows, heads)
    scores = einsum_wide('bihd,bjhd->bhij', query_heads, key_heads) * scale + block_bias.astype(jnp.float32)
    probs = softmax_rows(scores)
    probs_rounded = probs.astype(jnp.bfloat16)
    attended = einsum_wide('bhij,bjhd->bihd', probs_rounded, value_heads).reshape(block_count, row_count, width).astype(jnp.bfloat16)
    middle = (block_atoms.astype(jnp.float32) + project_rows(attended, w_out)).astype(jnp.bfloat16)
    cross_query = project_rows(middle, w_cquery).astype(jnp.bfloat16)
    cquery_heads = split_heads(cross_query, heads)
    ckey_heads = split_heads(cross_keys, heads)
    cvalue_heads = split_heads(cross_values, heads)
    cross_scores = einsum_wide('bihd,bthd->bhit', cquery_heads, ckey_heads) * scale + cross_bias.astype(jnp.float32)[:, :, None, :]
    cross_probs = softmax_rows(cross_scores)
    cross_rounded = cross_probs.astype(jnp.bfloat16)
    cross_attended = einsum_wide('bhit,bthd->bihd', cross_rounded, cvalue_heads).reshape(block_count, row_count, width).astype(jnp.bfloat16)
    updated = (middle.astype(jnp.float32) + project_rows(cross_attended, w_cout)).astype(jnp.bfloat16)
    grad_cout = weight_product(cross_attended, cotangent_rows)
    d_cross = project_back(cotangent_rows, w_cout).astype(jnp.bfloat16)
    d_cross_probs = einsum_wide('bihd,bthd->bhit', split_heads(d_cross, heads), cvalue_heads)
    d_cross_scores = (cross_probs * (d_cross_probs - lax.optimization_barrier(jnp.sum(cross_probs * d_cross_probs, axis=-1, keepdims=True))) * scale).astype(jnp.bfloat16)
    d_cross_query = einsum_wide('bhit,bthd->bihd', d_cross_scores, ckey_heads).reshape(block_count, row_count, width).astype(jnp.bfloat16)
    grad_cquery = weight_product(middle, d_cross_query)
    d_middle = (cotangent_rows.astype(jnp.float32) + project_back(d_cross_query, w_cquery)).astype(jnp.bfloat16)
    grad_out = weight_product(attended, d_middle)
    d_attended = project_back(d_middle, w_out).astype(jnp.bfloat16)
    dattn_heads = split_heads(d_attended, heads)
    d_probs = einsum_wide('bihd,bjhd->bhij', dattn_heads, value_heads)
    d_scores = (probs * (d_probs - lax.optimization_barrier(jnp.sum(probs * d_probs, axis=-1, keepdims=True))) * scale).astype(jnp.bfloat16)
    d_query = einsum_wide('bhij,bjhd->bihd', d_scores, key_heads).reshape(block_count, row_count, width).astype(jnp.bfloat16)
    d_key = einsum_wide('bhij,bihd->bjhd', d_scores, query_heads).reshape(block_count, row_count, width).astype(jnp.bfloat16)
    d_value = einsum_wide('bhij,bihd->bjhd', probs_rounded, dattn_heads).reshape(block_count, row_count, width).astype(jnp.bfloat16)
    grad_query = weight_product(block_atoms, d_query)
    grad_key = weight_product(block_atoms, d_key)
    grad_value = weight_product(block_atoms, d_value)
    grads = jnp.stack([grad_query, grad_key, grad_value, grad_out, grad_cquery, grad_cout])
    return (updated, grads)

def reference(atoms, distance_bins, bonds, molecule, block_counts, block_scaffold, pocket_ids, pocket_keys, pocket_values, pocket_bias, bin_table, bond_weight, w_query, w_key, w_value, w_out, w_cross_query, w_cross_out, cotangent):
    counts = block_counts.astype(jnp.int32)
    ends = jnp.cumsum(counts, axis=0).astype(jnp.int32)
    starts = (ends - counts).astype(jnp.int32)
    block_index = jnp.arange(BLOCKS, dtype=jnp.int32)
    target_device = block_index // (POCKET_DEVS * BAL)
    group_index = block_index // BAL % POCKET_DEVS
    live_rank = block_index % BAL * DP_DEVS + target_device
    source_device = lax.optimization_barrier(jnp.sum((ends[:, group_index] <= live_rank[None, :]).astype(jnp.int32), axis=0)).astype(jnp.int32)
    source_slot = ((source_device * POCKET_DEVS + group_index) * CAP + live_rank - starts[source_device, group_index]).astype(jnp.int32)
    key_blocks = pocket_keys.reshape(PBLK, A, D)
    value_blocks = pocket_values.reshape(PBLK, A, D)
    bias_blocks = pocket_bias.reshape(H, PBLK, A)
    weights = (w_query, w_key, w_value, w_out, w_cross_query, w_cross_out)

    def one_device(total, inputs):
        slot_rows, cotangent_rows = inputs
        block_bias = pair_bias(distance_bins[slot_rows], bonds[slot_rows], molecule[slot_rows], bin_table, bond_weight)
        chosen = pocket_ids[block_scaffold[slot_rows]]
        cross_keys = key_blocks[chosen].reshape(BAL, KP * A, D)
        cross_values = value_blocks[chosen].reshape(BAL, KP * A, D)
        cross_bias = jnp.transpose(bias_blocks[:, chosen], (1, 0, 2, 3)).reshape(BAL, H, KP * A)
        updated, grads = layer_pass(atoms[slot_rows], block_bias, cross_keys, cross_values, cross_bias, cotangent_rows, weights, H)
        return (total + grads, updated)
    total, updated = lax.scan(one_device, jnp.zeros((6, D, D), jnp.float32), (source_slot.reshape(-1, BAL), cotangent.reshape(-1, BAL, A, D)))
    weight_grads = (total * (1.0 / math.sqrt(ROWS))).astype(jnp.bfloat16)
    return (updated.reshape(BLOCKS, A, D), weight_grads)
```

```python
import math

import jax
import jax.numpy as jnp
from jax import lax
from jax.experimental import pallas as pl
from jax.experimental.pallas import tpu as pltpu
from jax.sharding import Mesh
from jax.sharding import PartitionSpec as P

masked_value = -30000.0
f32, bf16 = jnp.float32, jnp.bfloat16
A, D, H = 128, 768, 12
PAIRS = 6
NB = 4
T = 512
HALF = D // 2


def mm(a, b):
    return lax.dot_general(a, b, (((1,), (0,)), ((), ())), preferred_element_type=f32)


def mm_t(a, b):
    return lax.dot_general(a, b, (((1,), (1,)), ((), ())), preferred_element_type=f32)


def mm_l(a, b):
    return lax.dot_general(a, b, (((0,), (0,)), ((), ())), preferred_element_type=f32)


def low_lanes():
    return lax.broadcasted_iota(jnp.int32, (A, A), 1) < A // 2


def stack_heads(pair, low):
    zero = jnp.zeros_like(pair)
    return jnp.concatenate([jnp.where(low, pair, zero), jnp.where(low, zero, pair)], axis=0)


def join_heads(both, low):
    return jnp.where(low, both[:A], both[A:])


def softmax(s):
    e = jnp.exp(s - jnp.max(s, axis=-1, keepdims=True))
    return e * pl.reciprocal(jnp.sum(e, axis=-1, keepdims=True))


def cols(p):
    return slice(p * A, (p + 1) * A)


def self_kernel(src, slot, got, mol, table, w_q, w_k, w_v, w_o, w_cq, w_co, cot,
                x_o, q_o, k_o, v_o, p_o, at_o, mid_o, cq_o, dc_o, buf, idx, sems):
    for b in range(NB):
        pltpu.make_async_copy(got.at[src[b]], buf.at[b], sems.at[b]).start()
    dc_o[...] = mm_t(cot[...], w_co[...]).astype(bf16)
    for b in range(NB):
        pltpu.make_async_copy(got.at[src[b]], buf.at[b], sems.at[b]).wait()
        rows = slice(b * A, (b + 1) * A)
        x_o[rows, :] = buf[b, :, :D]
        bins = buf[b, :, D:D + A].astype(f32).astype(jnp.int32)
        bond = buf[b, :, D + A:].astype(f32).astype(jnp.int32)
        own = jnp.broadcast_to(mol[pl.ds(src[b] * 8 + slot[b], 1), :].astype(f32), (A, A))
        idx[b] = jnp.where(own == own.T, bins + 32 * bond, 64)
    x = x_o[...]
    q_o[...] = mm(x, w_q[...]).astype(bf16) * 0.125
    k_o[...] = mm(x, w_k[...]).astype(bf16)
    v_o[...] = mm(x, w_v[...]).astype(bf16)
    low = low_lanes()

    def block(b, carry):
        rows = pl.ds(pl.multiple_of(b * A, A), A)
        codes = idx[b]
        for p in range(PAIRS):
            s = mm_t(stack_heads(q_o[rows, cols(p)], low), k_o[rows, cols(p)])
            bias = [
                jnp.take_along_axis(jnp.broadcast_to(table[2 * p + h:2 * p + h + 1, :], (A, A)), codes, axis=1)
                for h in range(2)
            ]
            probs = softmax(s + jnp.concatenate(bias, axis=0))
            p_o[b, p] = probs
            o = mm(probs.astype(bf16), v_o[rows, cols(p)])
            at_o[rows, cols(p)] = join_heads(o, low).astype(bf16)
        return carry

    lax.fori_loop(0, NB, block, 0)
    mid = (x.astype(f32) + mm(at_o[...], w_o[...])).astype(bf16)
    mid_o[...] = mid
    cq_o[...] = mm(mid, w_cq[...]).astype(bf16) * 0.125


def cross_kernel(chosen, me, *refs):
    near, far = refs[:8], refs[8:16]
    (cq, dc, mid, at, cot, w_co, w_cq, w_o, up_o, da_o, keep_o, send_o, pocket, ca, dcq, sems) = refs[16:]
    x, yh, c = me[0], me[1], me[2]

    def copies():
        out = []
        for i in range(8):
            group = ((x + 4 - i // 2) % 4) * 2 + (yh + i) % 2
            out.append(pltpu.make_async_copy(near[i], pocket.at[group * 2 + c], sems.at[i]))
            out.append(pltpu.make_async_copy(far[i], pocket.at[group * 2 + 1 - c], sems.at[8 + i]))
        return out

    for copy in copies():
        copy.start()
    low = low_lanes()
    for copy in copies():
        copy.wait()

    def block(b, carry):
        rows = pl.ds(pl.multiple_of(b * A, A), A)
        names = [chosen[b * 4 + t] for t in range(4)]
        for p in range(PAIRS):
            kk = jnp.concatenate([pocket[n, :A, cols(p)] for n in names], axis=0)
            vv = jnp.concatenate([pocket[n, :A, cols(PAIRS + p)] for n in names], axis=0)
            s = mm_t(stack_heads(cq[rows, cols(p)], low), kk)
            bb = [
                jnp.broadcast_to(
                    jnp.concatenate([pocket[n, A:A + 1, cols(2 * p + h)] for n in names], axis=1).astype(f32), (A, T))
                for h in range(2)
            ]
            probs = softmax(s + jnp.concatenate(bb, axis=0))
            o = mm(probs.astype(bf16), vv)
            ca[rows, cols(p)] = join_heads(o, low).astype(bf16)
            dp = mm_t(stack_heads(dc[rows, cols(p)], low), vv)
            delta = jnp.sum(probs * dp, axis=-1, keepdims=True)
            ds = (probs * (dp - delta)).astype(bf16)
            dcq[rows, cols(p)] = (join_heads(mm(ds, kk), low) * 0.125).astype(bf16)
        return carry

    lax.fori_loop(0, NB, block, 0)
    up_o[...] = (mid[...].astype(f32) + mm(ca[...], w_co[...])).astype(bf16)
    dm = (cot[...].astype(f32) + mm_t(dcq[...], w_cq[...])).astype(bf16)
    da_o[...] = mm_t(dm, w_o[...]).astype(bf16)
    split_store(keep_o, send_o, 0, mm_l(at[...], dm).astype(bf16), c)
    split_store(keep_o, send_o, 1, mm_l(mid[...], dcq[...]).astype(bf16), c)
    split_store(keep_o, send_o, 2, mm_l(ca[...], cot[...]).astype(bf16), c)


def split_store(keep_o, send_o, i, full, c):
    lo, hi = full[:, :HALF], full[:, HALF:]

    @pl.when(c == 0)
    def _():
        keep_o[i] = lo
        send_o[i] = hi

    @pl.when(c == 1)
    def _():
        keep_o[i] = hi
        send_o[i] = lo


def back_kernel(me, x, q, k, v, probs, da, keep_o, send_o, dqkv):
    low = low_lanes()

    def block(b, carry):
        rows = pl.ds(pl.multiple_of(b * A, A), A)
        for p in range(PAIRS):
            dd = stack_heads(da[rows, cols(p)], low)
            dp = mm_t(dd, v[rows, cols(p)])
            pr = probs[b, p]
            delta = jnp.sum(pr * dp, axis=-1, keepdims=True)
            ds = (pr * (dp - delta)).astype(bf16)
            dqkv[rows, cols(p)] = (join_heads(mm(ds, k[rows, cols(p)]), low) * 0.125).astype(bf16)
            dqkv[rows, cols(6 + p)] = mm_l(ds, stack_heads(q[rows, cols(p)], low)).astype(bf16)
            dqkv[rows, cols(12 + p)] = mm_l(pr.astype(bf16), dd).astype(bf16)
        return carry

    lax.fori_loop(0, NB, block, 0)
    for i in range(3):
        split_store(keep_o, send_o, i, mm_l(x[...], dqkv[:, i * D:(i + 1) * D]).astype(bf16), me[2])


V = pl.BlockSpec(memory_space=pltpu.VMEM)
S = pl.BlockSpec(memory_space=pltpu.SMEM)
ANY = pl.BlockSpec(memory_space=pl.ANY)
R = NB * A


def sds(shape, dt=bf16):
    return jax.ShapeDtypeStruct(shape, dt)


def self_call(src, slot, got, mol, table, ws, cot):
    return pl.pallas_call(
        self_kernel,
        out_shape=[sds((R, D)) for _ in range(4)] + [sds((NB, PAIRS, 2 * A, A), f32)] + [sds((R, D)) for _ in range(4)],
        in_specs=[S, S, ANY] + [V] * 9,
        out_specs=[V] * 9,
        scratch_shapes=[pltpu.VMEM((NB, A, D + 2 * A), bf16), pltpu.VMEM((NB, A, A), jnp.int32),
                        pltpu.SemaphoreType.DMA((NB,))],
        name="self_forward",
    )(src, slot, got, mol, table, *ws, cot)


def cross_call(chosen, me, near, far, cq, dc, mid, at, cot, w_co, w_cq, w_o):
    return pl.pallas_call(
        cross_kernel,
        out_shape=[sds((R, D)), sds((R, D)), sds((3, D, HALF)), sds((3, D, HALF))],
        in_specs=[S, S] + [ANY] * 16 + [V] * 8,
        out_specs=[V] * 4,
        scratch_shapes=[pltpu.VMEM((16, A + 8, 2 * D), bf16), pltpu.VMEM((R, D), bf16), pltpu.VMEM((R, D), bf16),
                        pltpu.SemaphoreType.DMA((16,))],
        name="cross_both",
    )(chosen, me, *near, *far, cq, dc, mid, at, cot, w_co, w_cq, w_o)


def back_call(me, x, q, k, v, probs, da):
    return pl.pallas_call(
        back_kernel,
        out_shape=[sds((3, D, HALF)), sds((3, D, HALF))],
        in_specs=[S] + [V] * 6,
        out_specs=[V] * 2,
        scratch_shapes=[pltpu.VMEM((R, 3 * D), bf16)],
        name="self_backward",
    )(me, x, q, k, v, probs, da)


def pack_kernel(counts, me, atoms, bins, bonds, out):
    out[0, :, :D] = atoms[0]
    out[0, :, D:D + A] = bins[0].astype(f32).astype(bf16)
    out[0, :, D + A:] = bonds[0].astype(f32).astype(bf16)


def pack_call(counts, me, atoms, bins, bonds):
    def slot(t, counts, me):
        offset = sum(jnp.where(d < me[3], counts[d], 0) for d in range(8))
        return (t + 64 - offset) % 8, 0, 0

    return pl.pallas_call(
        pack_kernel,
        out_shape=sds((8, A, D + 2 * A)),
        grid_spec=pltpu.PrefetchScalarGridSpec(
            num_scalar_prefetch=2,
            grid=(8,),
            in_specs=[pl.BlockSpec((1, A, D), slot), pl.BlockSpec((1, A, A), slot), pl.BlockSpec((1, A, A), slot)],
            out_specs=pl.BlockSpec((1, A, D + 2 * A), lambda t, counts, me: (t, 0, 0)),
        ),
        name="pack_slots",
    )(counts, me, atoms, bins, bonds)


def index_kernel(counts, me, scaffold, ids, src_o, slot_o, chosen_o):
    dp, column = me[3], me[4]
    for b in range(NB):
        rank = b * 8 + dp
        source, begin, end = 0, 0, 0
        for d in range(8):
            end = end + counts[d]
            passed = (end <= rank).astype(jnp.int32)
            source = source + passed
            begin = jnp.where(passed == 1, end, begin)
        src_o[b] = source
        slot_o[b] = rank - begin
        name = scaffold[(source * 16 + column) * 8 + rank - begin]
        for t in range(4):
            chosen_o[b * 4 + t] = ids[t, name]


def index_call(counts, me, scaffold, ids):
    i32 = jnp.int32
    return pl.pallas_call(
        index_kernel,
        out_shape=[sds((NB,), i32), sds((NB,), i32), sds((NB * 4,), i32)],
        in_specs=[S] * 4,
        out_specs=[S] * 3,
        name="find_blocks",
    )(counts, me, scaffold, ids)


CHIPS = ("z", "yl", "x", "yh")


def exchange(matrix, axes):
    return lax.all_to_all(matrix, axes, split_axis=0, concat_axis=0, tiled=True)


def shifted(matrix, dx, dy):
    pairs = []
    for x in range(4):
        for y in range(2):
            pairs.append((x * 2 + y, (x + dx) % 4 * 2 + (y + dy) % 2))
    return lax.ppermute(matrix, ("x", "yh"), pairs)


def swap_core(matrix):
    return lax.ppermute(matrix, "c", [(0, 1), (1, 0)])


def reduce_grads(keep, send):
    half = (keep.astype(f32) + swap_core(send).astype(f32)).astype(bf16)
    pieces = exchange(half.reshape(64, -1, HALF), CHIPS)
    total = (jnp.sum(pieces.astype(f32), axis=0) * (1.0 / 256.0)).astype(bf16)
    return exchange(jnp.broadcast_to(total[None], pieces.shape), CHIPS).reshape(-1, D, HALF)


def on_device(
    atoms, distance_bins, bonds, molecule, block_counts, block_scaffold, pocket_ids, pocket_keys, pocket_values,
    pocket_bias, bin_table, bond_weight, w_query, w_key, w_value, w_out, w_cross_query, w_cross_out, cotangent,
):
    z, yl, x, yh, c = (lax.axis_index(n) for n in ("z", "yl", "x", "yh", "c"))
    me = jnp.stack([x, yh, c, z * 2 + yl, x * 4 + yh * 2 + c]).astype(jnp.int32)
    note = jnp.concatenate([molecule, jnp.broadcast_to(block_counts, (8, A))], axis=0)
    notes = exchange(jnp.broadcast_to(note[None], (8, 16, A)), ("z", "yl"))
    counts = notes[:, 8, 0]
    mol = notes[:, :8].reshape(64, A)
    got = exchange(pack_call(counts, me, atoms, distance_bins, bonds), ("z", "yl"))
    pocket = jnp.concatenate(
        [
            jnp.concatenate([pocket_keys, pocket_values], axis=1),
            jnp.broadcast_to(pocket_bias.reshape(1, 2 * D), (8, 2 * D)),
        ],
        axis=0,
    )
    near = [pocket if i == 0 else shifted(pocket, i // 2, i % 2) for i in range(8)]
    far = [swap_core(n) for n in near]
    src, slot, chosen = index_call(counts, me, block_scaffold, pocket_ids.T)
    table = jnp.concatenate(
        [
            bin_table,
            bin_table + bond_weight[:, None],
            jnp.full((H, A - 64), masked_value, f32),
        ],
        axis=1,
    )
    table = lax.reduce_precision(table, 8, 7)
    cot = cotangent.reshape(R, D)
    ws = (w_query, w_key, w_value, w_out, w_cross_query, w_cross_out)
    xs, q, k, v, probs, at, mid, cq, dc = self_call(src, slot, got, mol, table, ws, cot)
    updated, da, keep_a, send_a = cross_call(
        chosen, me, near, far, cq, dc, mid, at, cot, w_cross_out, w_cross_query, w_out
    )
    keep_b, send_b = back_call(me, xs, q, k, v, probs, da)
    mine = reduce_grads(jnp.concatenate([keep_b, keep_a]), jnp.concatenate([send_b, send_a]))
    theirs = swap_core(mine)
    low = jnp.where(c == 0, mine, theirs)
    high = jnp.where(c == 0, theirs, mine)
    return updated.reshape(cotangent.shape), jnp.concatenate([low, high], axis=2)


def solution(mesh):
    fine = Mesh(mesh.devices.reshape(4, 2, 4, 2, 2), ("z", "yl", "x", "yh", "c"))
    every = ("z", "yl", "x", "yh", "c")
    pocket = ("x", "yh", "c")
    return jax.shard_map(
        on_device,
        mesh=fine,
        in_specs=(
            P(every, None, None),
            P(every, None, None),
            P(every, None, None),
            P(every, None),
            P(("z", "yl"), pocket),
            P(),
            P(),
            P(pocket, None),
            P(pocket, None),
            P(None, pocket),
            P(),
            P(),
            P(),
            P(),
            P(),
            P(),
            P(),
            P(),
            P(every, None, None),
        ),
        out_specs=(P(every, None, None), P()),
        check_vma=False,
    )
```

```python
import jax
import jax.numpy as jnp
from jax import lax
from jax.experimental import pallas as pl
from jax.experimental.pallas import tpu as pltpu
from jax.sharding import Mesh
from jax.sharding import PartitionSpec as P

masked_value = -30000.0
f32, bf16 = jnp.float32, jnp.bfloat16
A, D, H = 128, 768, 12
PAIRS = 6
NB = 4
T = 512
HALF = D // 2


def mm(a, b):
    return lax.dot_general(a, b, (((1,), (0,)), ((), ())), preferred_element_type=f32)


def mm_t(a, b):
    return lax.dot_general(a, b, (((1,), (1,)), ((), ())), preferred_element_type=f32)


def mm_l(a, b):
    return lax.dot_general(a, b, (((0,), (0,)), ((), ())), preferred_element_type=f32)


def low_lanes():
    return lax.broadcasted_iota(jnp.int32, (A, A), 1) < A // 2


def stack_heads(pair, low):
    zero = jnp.zeros_like(pair)
    return jnp.concatenate([jnp.where(low, pair, zero), jnp.where(low, zero, pair)], axis=0)


def join_heads(both, low):
    return jnp.where(low, both[:A], both[A:])


def softmax(s):
    e = jnp.exp(s - jnp.max(s, axis=-1, keepdims=True))
    return e * pl.reciprocal(jnp.sum(e, axis=-1, keepdims=True))


def cols(p):
    return slice(p * A, (p + 1) * A)


def self_kernel(src, slot, got, mol, table, w_q, w_k, w_v, w_o, w_cq, w_co, cot,
                x_o, q_o, k_o, v_o, p_o, at_o, mid_o, cq_o, dc_o, buf, idx, sems):
    for b in range(NB):
        pltpu.make_async_copy(got.at[src[b]], buf.at[b], sems.at[b]).start()
    dc_o[...] = mm_t(cot[...], w_co[...]).astype(bf16)
    for b in range(NB):
        pltpu.make_async_copy(got.at[src[b]], buf.at[b], sems.at[b]).wait()
        rows = slice(b * A, (b + 1) * A)
        x_o[rows, :] = buf[b, :, :D]
        bins = buf[b, :, D:D + A].astype(f32).astype(jnp.int32)
        bond = buf[b, :, D + A:].astype(f32).astype(jnp.int32)
        own = jnp.broadcast_to(mol[src[b], pl.ds(slot[b], 1), :].astype(f32), (A, A))
        idx[b] = jnp.where(own == own.T, bins + 32 * bond, 64)
    x = x_o[...]
    q_o[...] = mm(x, w_q[...]).astype(bf16) * 0.125
    k_o[...] = mm(x, w_k[...]).astype(bf16)
    v_o[...] = mm(x, w_v[...]).astype(bf16)
    low = low_lanes()

    def block(b, carry):
        rows = pl.ds(pl.multiple_of(b * A, A), A)
        codes = idx[b]
        for p in range(PAIRS):
            s = mm_t(stack_heads(q_o[rows, cols(p)], low), k_o[rows, cols(p)])
            bias = [
                jnp.take_along_axis(jnp.broadcast_to(table[2 * p + h:2 * p + h + 1, :], (A, A)), codes, axis=1)
                for h in range(2)
            ]
            probs = softmax(s + jnp.concatenate(bias, axis=0))
            p_o[b, p] = probs
            o = mm(probs.astype(bf16), v_o[rows, cols(p)])
            at_o[rows, cols(p)] = join_heads(o, low).astype(bf16)
        return carry

    lax.fori_loop(0, NB, block, 0)
    mid = (x.astype(f32) + mm(at_o[...], w_o[...])).astype(bf16)
    mid_o[...] = mid
    cq_o[...] = mm(mid, w_cq[...]).astype(bf16) * 0.125


def cross_kernel(chosen, me, *refs):
    near, far = refs[:8], refs[8:16]
    (cq, dc, mid, at, cot, w_co, w_cq, w_o, up_o, da_o, keep_o, send_o, pocket, ca, dcq, sems) = refs[16:]
    x, yh, c = me[0], me[1], me[2]

    def copies():
        out = []
        for i in range(8):
            group = ((x + 4 - i // 2) % 4) * 2 + (yh + i) % 2
            out.append(pltpu.make_async_copy(near[i], pocket.at[group * 2 + c], sems.at[i]))
            out.append(pltpu.make_async_copy(far[i], pocket.at[group * 2 + 1 - c], sems.at[8 + i]))
        return out

    for copy in copies():
        copy.start()
    low = low_lanes()
    for copy in copies():
        copy.wait()

    def block(b, carry):
        rows = pl.ds(pl.multiple_of(b * A, A), A)
        names = [chosen[b * 4 + t] for t in range(4)]
        for p in range(PAIRS):
            kk = jnp.concatenate([pocket[n, :A, cols(p)] for n in names], axis=0)
            vv = jnp.concatenate([pocket[n, :A, cols(PAIRS + p)] for n in names], axis=0)
            s = mm_t(stack_heads(cq[rows, cols(p)], low), kk)
            bb = [
                jnp.broadcast_to(
                    jnp.concatenate([pocket[n, A:A + 1, cols(2 * p + h)] for n in names], axis=1).astype(f32), (A, T))
                for h in range(2)
            ]
            probs = softmax(s + jnp.concatenate(bb, axis=0))
            o = mm(probs.astype(bf16), vv)
            ca[rows, cols(p)] = join_heads(o, low).astype(bf16)
            dp = mm_t(stack_heads(dc[rows, cols(p)], low), vv)
            delta = jnp.sum(probs * dp, axis=-1, keepdims=True)
            ds = (probs * (dp - delta)).astype(bf16)
            dcq[rows, cols(p)] = (join_heads(mm(ds, kk), low) * 0.125).astype(bf16)
        return carry

    lax.fori_loop(0, NB, block, 0)
    up_o[...] = (mid[...].astype(f32) + mm(ca[...], w_co[...])).astype(bf16)
    dm = (cot[...].astype(f32) + mm_t(dcq[...], w_cq[...])).astype(bf16)
    da_o[...] = mm_t(dm, w_o[...]).astype(bf16)
    split_store(keep_o, send_o, 0, mm_l(at[...], dm).astype(bf16), c)
    split_store(keep_o, send_o, 1, mm_l(mid[...], dcq[...]).astype(bf16), c)
    split_store(keep_o, send_o, 2, mm_l(ca[...], cot[...]).astype(bf16), c)


def split_store(keep_o, send_o, i, full, c):
    lo, hi = full[:, :HALF], full[:, HALF:]

    @pl.when(c == 0)
    def _():
        keep_o[i] = lo
        send_o[i] = hi

    @pl.when(c == 1)
    def _():
        keep_o[i] = hi
        send_o[i] = lo


def back_kernel(me, x, q, k, v, probs, da, keep_o, send_o, dqkv):
    low = low_lanes()

    def block(b, carry):
        rows = pl.ds(pl.multiple_of(b * A, A), A)
        for p in range(PAIRS):
            dd = stack_heads(da[rows, cols(p)], low)
            dp = mm_t(dd, v[rows, cols(p)])
            pr = probs[b, p]
            delta = jnp.sum(pr * dp, axis=-1, keepdims=True)
            ds = (pr * (dp - delta)).astype(bf16)
            dqkv[rows, cols(p)] = (join_heads(mm(ds, k[rows, cols(p)]), low) * 0.125).astype(bf16)
            dqkv[rows, cols(6 + p)] = mm_l(ds, stack_heads(q[rows, cols(p)], low)).astype(bf16)
            dqkv[rows, cols(12 + p)] = mm_l(pr.astype(bf16), dd).astype(bf16)
        return carry

    lax.fori_loop(0, NB, block, 0)
    for i in range(3):
        split_store(keep_o, send_o, i, mm_l(x[...], dqkv[:, i * D:(i + 1) * D]).astype(bf16), me[2])


V = pl.BlockSpec(memory_space=pltpu.VMEM)
S = pl.BlockSpec(memory_space=pltpu.SMEM)
ANY = pl.BlockSpec(memory_space=pl.ANY)
R = NB * A


def sds(shape, dt=bf16):
    return jax.ShapeDtypeStruct(shape, dt)


def self_call(src, slot, got, mol, table, ws, cot):
    return pl.pallas_call(
        self_kernel,
        out_shape=[sds((R, D)) for _ in range(4)] + [sds((NB, PAIRS, 2 * A, A), f32)] + [sds((R, D)) for _ in range(4)],
        in_specs=[S, S, ANY] + [V] * 9,
        out_specs=[V] * 9,
        scratch_shapes=[pltpu.VMEM((NB, A, D + 2 * A), bf16), pltpu.VMEM((NB, A, A), jnp.int32),
                        pltpu.SemaphoreType.DMA((NB,))],
        cost_estimate=pl.CostEstimate(flops=16_000_000_000, transcendentals=0, bytes_accessed=8_000_000),
        name="self_forward",
    )(src, slot, got, mol, table, *ws, cot)


def cross_call(chosen, me, near, far, cq, dc, mid, at, cot, w_co, w_cq, w_o):
    return pl.pallas_call(
        cross_kernel,
        out_shape=[sds((R, D)), sds((R, D)), sds((3, D, HALF)), sds((3, D, HALF))],
        in_specs=[S, S] + [ANY] * 16 + [V] * 8,
        out_specs=[V] * 4,
        scratch_shapes=[pltpu.VMEM((16, A + 8, 2 * D), bf16), pltpu.VMEM((R, D), bf16), pltpu.VMEM((R, D), bf16),
                        pltpu.SemaphoreType.DMA((16,))],
        cost_estimate=pl.CostEstimate(flops=28_000_000_000, transcendentals=0, bytes_accessed=8_000_000),
        name="cross_both",
    )(chosen, me, *near, *far, cq, dc, mid, at, cot, w_co, w_cq, w_o)


def back_call(me, x, q, k, v, probs, da):
    return pl.pallas_call(
        back_kernel,
        out_shape=[sds((3, D, HALF)), sds((3, D, HALF))],
        in_specs=[S] + [V] * 6,
        out_specs=[V] * 2,
        scratch_shapes=[pltpu.VMEM((R, 3 * D), bf16)],
        cost_estimate=pl.CostEstimate(flops=16_000_000_000, transcendentals=0, bytes_accessed=8_000_000),
        name="self_backward",
    )(me, x, q, k, v, probs, da)


def pack_kernel(atoms, bins, bonds, out):
    out[0, :, :D] = atoms[0]
    out[0, :, D:D + A] = bins[0].astype(f32).astype(bf16)
    out[0, :, D + A:] = bonds[0].astype(f32).astype(bf16)


def pack_call(atoms, bins, bonds):
    def slot(t):
        return t, 0, 0

    return pl.pallas_call(
        pack_kernel,
        out_shape=sds((8, A, D + 2 * A)),
        grid=(8,),
        in_specs=[pl.BlockSpec((1, A, D), slot), pl.BlockSpec((1, A, A), slot), pl.BlockSpec((1, A, A), slot)],
        out_specs=pl.BlockSpec((1, A, D + 2 * A), slot),
        name="pack_slots",
    )(atoms, bins, bonds)


def roll_kernel(counts, me, packed, out, sems):
    offset = 0
    for d in range(8):
        offset = offset + jnp.where(d < me[3], counts[d, 8, 0], 0)
    copies = [
        pltpu.make_async_copy(packed.at[(t + 64 - offset) % 8], out.at[t], sems.at[t])
        for t in range(8)
    ]
    for copy in copies:
        copy.start()
    for copy in copies:
        copy.wait()


def roll_call(counts, me, packed):
    return pl.pallas_call(
        roll_kernel,
        out_shape=sds((8, A, D + 2 * A)),
        in_specs=[S, S, ANY],
        out_specs=ANY,
        scratch_shapes=[pltpu.SemaphoreType.DMA((8,))],
        name="roll_slots",
    )(counts, me, packed)


def index_kernel(counts, me, scaffold, ids, src_o, slot_o, chosen_o):
    dp, column = me[3], me[4]
    for b in range(NB):
        rank = b * 8 + dp
        source, begin, end = 0, 0, 0
        for d in range(8):
            end = end + counts[d, 8, 0]
            passed = (end <= rank).astype(jnp.int32)
            source = source + passed
            begin = jnp.where(passed == 1, end, begin)
        src_o[b] = source
        slot_o[b] = rank - begin
        name = scaffold[(source * 16 + column) * 8 + rank - begin]
        for t in range(4):
            chosen_o[b * 4 + t] = ids[t, name]


def index_call(counts, me, scaffold, ids):
    i32 = jnp.int32
    return pl.pallas_call(
        index_kernel,
        out_shape=[sds((NB,), i32), sds((NB,), i32), sds((NB * 4,), i32)],
        in_specs=[S] * 4,
        out_specs=[S] * 3,
        name="find_blocks",
    )(counts, me, scaffold, ids)


def join_kernel(me, mine, theirs, out):
    @pl.when(me[2] == 0)
    def _():
        out[0, :, :HALF] = mine[0]
        out[0, :, HALF:] = theirs[0]

    @pl.when(me[2] == 1)
    def _():
        out[0, :, :HALF] = theirs[0]
        out[0, :, HALF:] = mine[0]


def join_call(me, mine, theirs):
    half = pl.BlockSpec((1, D, HALF), lambda i, me: (i, 0, 0))
    return pl.pallas_call(
        join_kernel,
        out_shape=sds((6, D, D)),
        grid_spec=pltpu.PrefetchScalarGridSpec(
            num_scalar_prefetch=1,
            grid=(6,),
            in_specs=[half, half],
            out_specs=pl.BlockSpec((1, D, D), lambda i, me: (i, 0, 0)),
        ),
        name="join_halves",
    )(me, mine, theirs)


CHIPS = ("z", "yl", "x", "yh")


def exchange(matrix, axes):
    return lax.all_to_all(matrix, axes, split_axis=0, concat_axis=0, tiled=True)


def shifted(matrix, dx, dy):
    pairs = []
    for x in range(4):
        for y in range(2):
            pairs.append((x * 2 + y, (x + dx) % 4 * 2 + (y + dy) % 2))
    return lax.ppermute(matrix, ("x", "yh"), pairs)


def swap_core(matrix):
    return lax.ppermute(matrix, "c", [(0, 1), (1, 0)])


def reduce_grads(keep, send):
    half = (keep.astype(f32) + swap_core(send).astype(f32)).astype(bf16)
    pieces = exchange(half.reshape(64, -1, HALF), CHIPS)
    total = (jnp.sum(pieces.astype(f32), axis=0) * (1.0 / 256.0)).astype(bf16)
    return exchange(jnp.broadcast_to(total[None], pieces.shape), CHIPS).reshape(-1, D, HALF)


def layer(
    atoms, distance_bins, bonds, molecule, block_counts, block_scaffold, pocket_ids, pocket_keys, pocket_values,
    pocket_bias, bin_table, bond_weight, w_query, w_key, w_value, w_out, w_cross_query, w_cross_out, cotangent,
):
    z, yl, x, yh, c = (lax.axis_index(n) for n in ("z", "yl", "x", "yh", "c"))
    me = jnp.stack([x, yh, c, z * 2 + yl, x * 4 + yh * 2 + c]).astype(jnp.int32)
    note = jnp.concatenate([molecule, jnp.broadcast_to(block_counts, (8, A))], axis=0)
    notes = exchange(jnp.broadcast_to(note[None], (8, 16, A)), ("z", "yl"))
    packed = pack_call(atoms, distance_bins, bonds)
    rolled = roll_call(notes, me, packed)
    got = exchange(rolled, ("z", "yl"))
    pocket = jnp.concatenate(
        [
            jnp.concatenate([pocket_keys, pocket_values], axis=1),
            jnp.broadcast_to(pocket_bias.reshape(1, 2 * D), (8, 2 * D)),
        ],
        axis=0,
    )
    mirror = shifted(pocket, 0, 1)
    near = [pocket, mirror]
    for i in range(1, 4):
        near.append(shifted(pocket, i, 0))
        near.append(shifted(mirror, i, 0))
    far = []
    for i in range(8):
        far.append(swap_core(near[i]))
    src, slot, chosen = index_call(notes, me, block_scaffold, pocket_ids.T)
    table = jnp.concatenate(
        [
            bin_table,
            bin_table + bond_weight[:, None],
            jnp.full((H, A - 64), masked_value, f32),
        ],
        axis=1,
    )
    table = lax.reduce_precision(table, 8, 7)
    cot = cotangent.reshape(R, D)
    ws = (w_query, w_key, w_value, w_out, w_cross_query, w_cross_out)
    xs, q, k, v, probs, at, mid, cq, dc = self_call(src, slot, got, notes, table, ws, cot)
    updated, da, keep_a, send_a = cross_call(
        chosen, me, near, far, cq, dc, mid, at, cot, w_cross_out, w_cross_query, w_out
    )
    keep_b, send_b = back_call(me, xs, q, k, v, probs, da)
    mine = reduce_grads(jnp.concatenate([keep_b, keep_a]), jnp.concatenate([send_b, send_a]))
    theirs = swap_core(mine)
    return updated.reshape(cotangent.shape), join_call(me, mine, theirs)


def solution(mesh):
    fine = Mesh(mesh.devices.reshape(4, 2, 4, 2, 2), ("z", "yl", "x", "yh", "c"))
    every = ("z", "yl", "x", "yh", "c")
    pocket = ("x", "yh", "c")
    return jax.shard_map(
        layer,
        mesh=fine,
        in_specs=(
            P(every, None, None),
            P(every, None, None),
            P(every, None, None),
            P(every, None),
            P(("z", "yl"), pocket),
            P(),
            P(),
            P(pocket, None),
            P(pocket, None),
            P(None, pocket),
            P(),
            P(),
            P(),
            P(),
            P(),
            P(),
            P(),
            P(),
            P(every, None, None),
        ),
        out_specs=(P(every, None, None), P()),
        check_vma=False,
    )
```

```python
import jax
import jax.numpy as jnp
from jax import lax
from jax.experimental import pallas as pl
from jax.experimental.pallas import tpu as pltpu
from jax.sharding import Mesh
from jax.sharding import PartitionSpec as P

masked_value = -30000.0
f32, bf16 = jnp.float32, jnp.bfloat16
A, D, H = 128, 768, 12
PAIRS = 6
NB = 4
T = 512
HALF = D // 2
ROWS = D // 4


def mm(a, b):
    return lax.dot_general(a, b, (((1,), (0,)), ((), ())), preferred_element_type=f32)


def mm_t(a, b):
    return lax.dot_general(a, b, (((1,), (1,)), ((), ())), preferred_element_type=f32)


def mm_l(a, b):
    return lax.dot_general(a, b, (((0,), (0,)), ((), ())), preferred_element_type=f32)


def low_lanes():
    return lax.broadcasted_iota(jnp.int32, (A, A), 1) < A // 2


def stack_heads(pair, low):
    zero = jnp.zeros_like(pair)
    return jnp.concatenate([jnp.where(low, pair, zero), jnp.where(low, zero, pair)], axis=0)


def join_heads(both, low):
    return jnp.where(low, both[:A], both[A:])


def softmax(s):
    e = jnp.exp(s - jnp.max(s, axis=-1, keepdims=True))
    return e * pl.reciprocal(jnp.sum(e, axis=-1, keepdims=True))


def cols(p):
    return slice(p * A, (p + 1) * A)


def self_kernel(src, slot, got, mol, table, w_q, w_k, w_v, w_o, w_cq, w_co, cot,
                x_o, q_o, k_o, v_o, p_o, at_o, mid_o, cq_o, dc_o, buf, idx, sems):
    for b in range(NB):
        pltpu.make_async_copy(got.at[src[b]], buf.at[b], sems.at[b]).start()
    dc_o[...] = mm_t(cot[...], w_co[...]).astype(bf16)
    for b in range(NB):
        pltpu.make_async_copy(got.at[src[b]], buf.at[b], sems.at[b]).wait()
        rows = slice(b * A, (b + 1) * A)
        x_o[rows, :] = buf[b, :, :D]
        bins = buf[b, :, D:D + A].astype(f32).astype(jnp.int32)
        bond = buf[b, :, D + A:].astype(f32).astype(jnp.int32)
        own = jnp.broadcast_to(mol[src[b], pl.ds(slot[b], 1), :].astype(f32), (A, A))
        idx[b] = jnp.where(own == own.T, bins + 32 * bond, 64)
    x = x_o[...]
    q_o[...] = mm(x, w_q[...]).astype(bf16) * 0.125
    k_o[...] = mm(x, w_k[...]).astype(bf16)
    v_o[...] = mm(x, w_v[...]).astype(bf16)
    low = low_lanes()

    def block(b, carry):
        rows = pl.ds(pl.multiple_of(b * A, A), A)
        codes = idx[b]
        for p in range(PAIRS):
            s = mm_t(stack_heads(q_o[rows, cols(p)], low), k_o[rows, cols(p)])
            bias = [
                jnp.take_along_axis(jnp.broadcast_to(table[2 * p + h:2 * p + h + 1, :], (A, A)), codes, axis=1)
                for h in range(2)
            ]
            probs = softmax(s + jnp.concatenate(bias, axis=0))
            p_o[b, p] = probs
            o = mm(probs.astype(bf16), v_o[rows, cols(p)])
            at_o[rows, cols(p)] = join_heads(o, low).astype(bf16)
        return carry

    lax.fori_loop(0, NB, block, 0)
    mid = (x.astype(f32) + mm(at_o[...], w_o[...])).astype(bf16)
    mid_o[...] = mid
    cq_o[...] = mm(mid, w_cq[...]).astype(bf16) * 0.125


def cross_kernel(chosen, me, *refs):
    near, far = refs[:8], refs[8:16]
    (cq, dc, mid, at, cot, w_co, w_cq, w_o, up_o, da_o, keep_o, send_o, pocket, ca, dcq, sems) = refs[16:]
    x, yh, c = me[0], me[1], me[2]

    def copies():
        out = []
        for i in range(8):
            group = ((x + 4 - i // 2) % 4) * 2 + (yh + i) % 2
            out.append(pltpu.make_async_copy(near[i], pocket.at[group * 2 + c], sems.at[i]))
            out.append(pltpu.make_async_copy(far[i], pocket.at[group * 2 + 1 - c], sems.at[8 + i]))
        return out

    for copy in copies():
        copy.start()
    low = low_lanes()
    for copy in copies():
        copy.wait()

    def block(b, carry):
        rows = pl.ds(pl.multiple_of(b * A, A), A)
        names = [chosen[b * 4 + t] for t in range(4)]
        for p in range(PAIRS):
            kk = jnp.concatenate([pocket[n, :A, cols(p)] for n in names], axis=0)
            vv = jnp.concatenate([pocket[n, :A, cols(PAIRS + p)] for n in names], axis=0)
            s = mm_t(stack_heads(cq[rows, cols(p)], low), kk)
            bb = [
                jnp.broadcast_to(
                    jnp.concatenate([pocket[n, A:A + 1, cols(2 * p + h)] for n in names], axis=1).astype(f32), (A, T))
                for h in range(2)
            ]
            probs = softmax(s + jnp.concatenate(bb, axis=0))
            o = mm(probs.astype(bf16), vv)
            ca[rows, cols(p)] = join_heads(o, low).astype(bf16)
            dp = mm_t(stack_heads(dc[rows, cols(p)], low), vv)
            delta = jnp.sum(probs * dp, axis=-1, keepdims=True)
            ds = (probs * (dp - delta)).astype(bf16)
            dcq[rows, cols(p)] = (join_heads(mm(ds, kk), low) * 0.125).astype(bf16)
        return carry

    lax.fori_loop(0, NB, block, 0)
    up_o[...] = (mid[...].astype(f32) + mm(ca[...], w_co[...])).astype(bf16)
    dm = (cot[...].astype(f32) + mm_t(dcq[...], w_cq[...])).astype(bf16)
    da_o[...] = mm_t(dm, w_o[...]).astype(bf16)
    split_store(keep_o, send_o, 0, mm_l(at[...], dm).astype(bf16), c)
    split_store(keep_o, send_o, 1, mm_l(mid[...], dcq[...]).astype(bf16), c)
    split_store(keep_o, send_o, 2, mm_l(ca[...], cot[...]).astype(bf16), c)


def split_store(keep_o, send_o, i, full, c):
    lo, hi = full[:, :HALF], full[:, HALF:]

    @pl.when(c == 0)
    def _():
        keep_o[i] = lo
        send_o[i] = hi

    @pl.when(c == 1)
    def _():
        keep_o[i] = hi
        send_o[i] = lo


def back_kernel(me, x, q, k, v, probs, da, keep_o, send_o, dqkv):
    low = low_lanes()

    def block(b, carry):
        rows = pl.ds(pl.multiple_of(b * A, A), A)
        for p in range(PAIRS):
            dd = stack_heads(da[rows, cols(p)], low)
            dp = mm_t(dd, v[rows, cols(p)])
            pr = probs[b, p]
            delta = jnp.sum(pr * dp, axis=-1, keepdims=True)
            ds = (pr * (dp - delta)).astype(bf16)
            dqkv[rows, cols(p)] = (join_heads(mm(ds, k[rows, cols(p)]), low) * 0.125).astype(bf16)
            dqkv[rows, cols(6 + p)] = mm_l(ds, stack_heads(q[rows, cols(p)], low)).astype(bf16)
            dqkv[rows, cols(12 + p)] = mm_l(pr.astype(bf16), dd).astype(bf16)
        return carry

    lax.fori_loop(0, NB, block, 0)
    for i in range(3):
        split_store(keep_o, send_o, i, mm_l(x[...], dqkv[:, i * D:(i + 1) * D]).astype(bf16), me[2])


V = pl.BlockSpec(memory_space=pltpu.VMEM)
S = pl.BlockSpec(memory_space=pltpu.SMEM)
ANY = pl.BlockSpec(memory_space=pl.ANY)
R = NB * A


def sds(shape, dt=bf16):
    return jax.ShapeDtypeStruct(shape, dt)


def self_call(src, slot, got, mol, table, ws, cot):
    return pl.pallas_call(
        self_kernel,
        out_shape=[sds((R, D)) for _ in range(4)] + [sds((NB, PAIRS, 2 * A, A), f32)] + [sds((R, D)) for _ in range(4)],
        in_specs=[S, S, ANY] + [V] * 9,
        out_specs=[V] * 9,
        scratch_shapes=[pltpu.VMEM((NB, A, D + 2 * A), bf16), pltpu.VMEM((NB, A, A), jnp.int32),
                        pltpu.SemaphoreType.DMA((NB,))],
        cost_estimate=pl.CostEstimate(flops=16_000_000_000, transcendentals=0, bytes_accessed=8_000_000),
        name="self_forward",
    )(src, slot, got, mol, table, *ws, cot)


def cross_call(chosen, me, near, far, cq, dc, mid, at, cot, w_co, w_cq, w_o):
    return pl.pallas_call(
        cross_kernel,
        out_shape=[sds((R, D)), sds((R, D)), sds((3, D, HALF)), sds((3, D, HALF))],
        in_specs=[S, S] + [ANY] * 16 + [V] * 8,
        out_specs=[V] * 4,
        scratch_shapes=[pltpu.VMEM((16, A + 8, 2 * D), bf16), pltpu.VMEM((R, D), bf16), pltpu.VMEM((R, D), bf16),
                        pltpu.SemaphoreType.DMA((16,))],
        cost_estimate=pl.CostEstimate(flops=28_000_000_000, transcendentals=0, bytes_accessed=8_000_000),
        name="cross_both",
    )(chosen, me, *near, *far, cq, dc, mid, at, cot, w_co, w_cq, w_o)


def back_call(me, x, q, k, v, probs, da):
    return pl.pallas_call(
        back_kernel,
        out_shape=[sds((3, D, HALF)), sds((3, D, HALF))],
        in_specs=[S] + [V] * 6,
        out_specs=[V] * 2,
        scratch_shapes=[pltpu.VMEM((R, 3 * D), bf16)],
        cost_estimate=pl.CostEstimate(flops=16_000_000_000, transcendentals=0, bytes_accessed=8_000_000),
        name="self_backward",
    )(me, x, q, k, v, probs, da)


def roll_kernel(notes, me, atoms, codes, out, sems):
    offset = 0
    for d in range(8):
        offset = offset + jnp.where(d < me[3], notes[d, 8, 0], 0)
    copies = []
    for t in range(8):
        slot = (t + 64 - offset) % 8
        copies.append(pltpu.make_async_copy(atoms.at[slot], out.at[t, :, pl.ds(0, D)], sems.at[t]))
        copies.append(pltpu.make_async_copy(codes.at[slot], out.at[t, :, pl.ds(D, 2 * A)], sems.at[8 + t]))
    for copy in copies:
        copy.start()
    for copy in copies:
        copy.wait()


def roll_call(notes, me, atoms, codes):
    return pl.pallas_call(
        roll_kernel,
        out_shape=sds((8, A, D + 2 * A)),
        in_specs=[S, S, ANY, ANY],
        out_specs=V,
        scratch_shapes=[pltpu.SemaphoreType.DMA((16,))],
        name="roll_slots",
    )(notes, me, atoms, codes)


def index_kernel(counts, me, scaffold, ids, src_o, slot_o, chosen_o):
    dp, column = me[3], me[4]
    for b in range(NB):
        rank = b * 8 + dp
        source, begin, end = 0, 0, 0
        for d in range(8):
            end = end + counts[d, 8, 0]
            passed = (end <= rank).astype(jnp.int32)
            source = source + passed
            begin = jnp.where(passed == 1, end, begin)
        src_o[b] = source
        slot_o[b] = rank - begin
        name = scaffold[(source * 16 + column) * 8 + rank - begin]
        for t in range(4):
            chosen_o[b * 4 + t] = ids[t, name]


def index_call(counts, me, scaffold, ids):
    i32 = jnp.int32
    return pl.pallas_call(
        index_kernel,
        out_shape=[sds((NB,), i32), sds((NB,), i32), sds((NB * 4,), i32)],
        in_specs=[S] * 4,
        out_specs=[S] * 3,
        name="find_blocks",
    )(counts, me, scaffold, ids)


def fold_kernel(me, *refs):
    keep_b, keep_a, got_b, got_a = refs[:4]
    outs = refs[4:]
    for i in range(3):
        for shift in range(4):
            first = (me[5 + i] + shift) % 4 * ROWS

            def step(r, carry, first=first, out=outs[i * 4 + shift]):
                rows = pl.ds(pl.multiple_of(first + r * 32, 32), 32)
                to = pl.ds(pl.multiple_of(r * 32, 32), 32)
                for j, (keep, got) in enumerate(((keep_b, got_b), (keep_a, got_a))):
                    out[j, to, :] = (keep[i, rows, :].astype(f32) + got[i, rows, :].astype(f32)).astype(bf16)
                return carry

            lax.fori_loop(0, ROWS // 32, step, 0)


def fold_call(me, keep_b, keep_a, got_b, got_a):
    return pl.pallas_call(
        fold_kernel,
        out_shape=[sds((2, ROWS, HALF))] * 12,
        in_specs=[S] + [V] * 4,
        out_specs=[V] * 12,
        name="fold_cores",
    )(me, keep_b, keep_a, got_b, got_a)


def add_kernel(scale, a, b, c, d, out):
    def step(r, carry):
        at = (slice(None), pl.ds(pl.multiple_of(r * 32, 32), 32), slice(None))
        total = (a[at].astype(f32) + c[at].astype(f32)) + (b[at].astype(f32) + d[at].astype(f32))
        out[at] = (total * scale).astype(bf16)
        return carry

    lax.fori_loop(0, ROWS // 32, step, 0)


def add_call(parts, scale):
    return pl.pallas_call(
        lambda *refs: add_kernel(scale, *refs),
        out_shape=sds((2, ROWS, HALF)),
        in_specs=[V] * 4,
        out_specs=V,
        name="add_ring",
    )(*parts)


def join_kernel(me, *refs):
    mine, theirs, out, sems = refs[:12], refs[12:24], refs[24], refs[25]
    for core in range(2):
        @pl.when(me[2] == core)
        def _():
            copies = []
            for i in range(3):
                for shift in range(4):
                    rows = pl.ds(pl.multiple_of((me[5 + i] + 4 - shift) % 4 * ROWS, ROWS), ROWS)
                    for j in range(2):
                        k = i * 4 + shift
                        for n, (half, ref) in enumerate(((core, mine[k]), (1 - core, theirs[k]))):
                            copies.append(pltpu.make_async_copy(
                                ref.at[j], out.at[3 * j + i, rows, pl.ds(half * HALF, HALF)],
                                sems.at[(k * 2 + j) * 2 + n]))
            for copy in copies:
                copy.start()
            for copy in copies:
                copy.wait()


def join_call(me, mine, theirs):
    return pl.pallas_call(
        join_kernel,
        out_shape=sds((6, D, D)),
        in_specs=[S] + [ANY] * 24,
        out_specs=V,
        scratch_shapes=[pltpu.SemaphoreType.DMA((48,))],
        name="join_halves",
    )(me, *mine, *theirs)


RINGS = (("x",), ("yl", "yh"), ("z",))


def ring(matrix, axis, shift):
    place = (0, 2, 1, 3) if axis == 1 else (0, 1, 2, 3)
    return lax.ppermute(matrix, RINGS[axis], [(place[i], place[(i + shift) % 4]) for i in range(4)])


def exchange(matrix, axes):
    return lax.all_to_all(matrix, axes, split_axis=0, concat_axis=0, tiled=True)


def shifted(matrix, dx, dy):
    pairs = []
    for x in range(4):
        for y in range(2):
            pairs.append((x * 2 + y, (x + dx) % 4 * 2 + (y + dy) % 2))
    return lax.ppermute(matrix, ("x", "yh"), pairs)


def swap_core(matrix):
    return lax.ppermute(matrix, "c", [(0, 1), (1, 0)])


def reduce_grads(me, keep_b, keep_a, got_b, got_a):
    pieces = fold_call(me, keep_b, keep_a, got_b, got_a)
    totals = []
    for i in range(3):
        own = pieces[4 * i:4 * i + 4]
        totals.append(add_call([own[0]] + [ring(own[n], i, n) for n in range(1, 4)], 1.0))
    for stage in (1, 2):
        for i in range(3):
            got = [ring(totals[i], (i + stage) % 3, n) for n in range(1, 4)]
            totals[i] = add_call([totals[i]] + got, 1.0 if stage == 1 else 1.0 / 256.0)
    mine, theirs = [], []
    for i in range(3):
        mine += [totals[i]] + [ring(totals[i], i, n) for n in range(1, 4)]
    for piece in mine:
        theirs.append(swap_core(piece))
    return join_call(me, mine, theirs)


def layer(
    atoms, distance_bins, bonds, molecule, block_counts, block_scaffold, pocket_ids, pocket_keys, pocket_values,
    pocket_bias, bin_table, bond_weight, w_query, w_key, w_value, w_out, w_cross_query, w_cross_out, cotangent,
):
    z, yl, x, yh, c = (lax.axis_index(n) for n in ("z", "yl", "x", "yh", "c"))
    me = jnp.stack([x, yh, c, z * 2 + yl, x * 4 + yh * 2 + c, x, yh * 2 + yl, z]).astype(jnp.int32)
    note = jnp.concatenate([molecule, jnp.broadcast_to(block_counts, (8, A))], axis=0)
    notes = exchange(jnp.broadcast_to(note[None], (8, 16, A)), ("z", "yl"))
    codes = jnp.concatenate([distance_bins, bonds], axis=2).astype(bf16)
    rolled = roll_call(notes, me, atoms, codes)
    got = exchange(rolled, ("z", "yl"))
    pocket = jnp.concatenate(
        [
            jnp.concatenate([pocket_keys, pocket_values], axis=1),
            jnp.broadcast_to(pocket_bias.reshape(1, 2 * D), (8, 2 * D)),
        ],
        axis=0,
    )
    mirror = shifted(pocket, 0, 1)
    near = [pocket, mirror]
    for i in range(1, 4):
        near.append(shifted(pocket, i, 0))
        near.append(shifted(mirror, i, 0))
    far = []
    for i in range(8):
        far.append(swap_core(near[i]))
    src, slot, chosen = index_call(notes, me, block_scaffold, pocket_ids.T)
    table = jnp.concatenate(
        [
            bin_table,
            bin_table + bond_weight[:, None],
            jnp.full((H, A - 64), masked_value, f32),
        ],
        axis=1,
    )
    table = lax.reduce_precision(table, 8, 7)
    cot = cotangent.reshape(R, D)
    ws = (w_query, w_key, w_value, w_out, w_cross_query, w_cross_out)
    xs, q, k, v, probs, at, mid, cq, dc = self_call(src, slot, got, notes, table, ws, cot)
    updated, da, keep_a, send_a = cross_call(
        chosen, me, near, far, cq, dc, mid, at, cot, w_cross_out, w_cross_query, w_out
    )
    keep_b, send_b = back_call(me, xs, q, k, v, probs, da)
    got_a = swap_core(send_a)
    got_b = swap_core(send_b)
    grads = reduce_grads(me, keep_b, keep_a, got_b, got_a)
    return updated.reshape(cotangent.shape), grads


def solution(mesh):
    fine = Mesh(mesh.devices.reshape(4, 2, 4, 2, 2), ("z", "yl", "x", "yh", "c"))
    every = ("z", "yl", "x", "yh", "c")
    pocket = ("x", "yh", "c")
    return jax.shard_map(
        layer,
        mesh=fine,
        in_specs=(
            P(every, None, None),
            P(every, None, None),
            P(every, None, None),
            P(every, None),
            P(("z", "yl"), pocket),
            P(),
            P(),
            P(pocket, None),
            P(pocket, None),
            P(None, pocket),
            P(),
            P(),
            P(),
            P(),
            P(),
            P(),
            P(),
            P(),
            P(every, None, None),
        ),
        out_specs=(P(every, None, None), P()),
        check_vma=False,
    )
```
